128 devices in a mesh: tok: 8 (over y, core), head: 16 (over x, z).
Axes of the slice: x: 4, y: 4, z: 4, core: 2. Of those that a mesh axis runs over, the one named last changes fastest.
Arguments:
- hidden_states: bfloat16 [5120, 6144], P('tok', 'head'), may hold values from -6 to 6
- norm_gain: float32 [6144], replicated, may hold values from 0.5 to 1.5
- norm_bias: float32 [6144], replicated, may hold values from -2 to 2
- qkv_weight: bfloat16 [6144, 18432], P('tok', 'head'), may hold values from -0.125 to 0.125
- qkv_bias: bfloat16 [18432], P('head'), may hold values from -2 to 2
- dense_weight: bfloat16 [6144, 6144], P('head'), may hold values from -0.21875 to 0.21875
- dense_bias: bfloat16 [6144], P('head'), may hold values from -2 to 2
- prefix_keys: bfloat16 [16, 2048, 6144], P('tok', None, 'head'), may hold values from -70 to 70
- prefix_values: bfloat16 [16, 2048, 6144], P('tok', None, 'head'), may hold values from -10 to 10
- suffix_len: int32 [8, 16], P('tok'), may hold values from 1 to 120, as said below
- request_order: int32 [8, 16], P('tok'), may hold values from 0 to 15, each once within a row
- group_slot: int32 [16], replicated, may hold values from 0 to 15, each once
Outputs:
- layer_out: bfloat16 [5120, 6144], P('tok', 'head')
The draws below stay inside these ranges and needn't reach their ends.
Inputs may be any that keep to these rules, and one draw needn't show every extreme that they name: `suffix_len`: each row sums to 640; one group, the same in every row, has exactly 120 in every row. `request_order`: each row names every group once. `group_slot`: each slot holds one group.
All inputs are finite; a program needn't handle non-finite values.
Results may differ from the reference program's by a relative error of at most 0.007.
The reference program's roundings to bfloat16 on the way count: a program that leaves them out, or rounds other values in their place, can miss the bound.
Values may be sent and summed in bfloat16 or wider, within the bound.
A program may use at most 128 MiB of HBM per device.

```python
import math
import jax
import jax.numpy as jnp
from jax import lax

D = 6144
HEADS = 64
HS = 96
ROT = 24
TOK_DEV = 640
PREFIX = 2048
GROUPS = 16
CAP = 120
TOKENS = 5120
N_TOK = 8


def draw_prefix_keys(key, part):
    base_key = jax.random.fold_in(key, 0)
    full_shape = (GROUPS, PREFIX, D)
    drawn = jax.random.normal(base_key, full_shape, jnp.float32)
    return drawn.astype(jnp.bfloat16)


def draw_suffix_len(key, part):
    heaviest_key, weight_key = jax.random.split(key)
    heaviest = jax.random.randint(heaviest_key, (), 0, GROUPS)
    labels = jnp.arange(GROUPS, dtype=jnp.int32)[None, :]
    weights = jax.random.randint(weight_key, (N_TOK, GROUPS), 2, 6)
    weights = jnp.where(labels == heaviest, 0, weights)
    surplus = TOK_DEV - CAP - (GROUPS - 1)
    shares = weights * surplus // jnp.sum(weights, axis=1, keepdims=True)
    leftover = surplus - jnp.sum(shares, axis=1, keepdims=True)
    ranking = labels - (labels > heaviest).astype(jnp.int32)
    extra_one = ((ranking < leftover) & (labels != heaviest)).astype(jnp.int32)
    return jnp.where(labels == heaviest, CAP, 1 + shares + extra_one).astype(jnp.int32)


def with_spikes(values, key, source, target, blocks, factor):
    owner, partner = [(jnp.arange(values.shape[axis_at]) // (values.shape[axis_at] // blocks)).reshape([-1 if axis == axis_at else 1 for axis in range(values.ndim)]) for axis_at in (source, target)]
    chosen = jax.random.permutation(key, blocks)[partner]
    strong = (owner == chosen) | (owner == (partner + blocks // 2) % blocks)
    return jnp.where(strong, factor * values, values)


def shard_levels(rng, shape, shards, smallest, largest):
    def one(dim, blocks):
        steps = jax.random.uniform(jax.random.fold_in(jax.random.fold_in(rng, 6), dim), (blocks,), jnp.float32, smallest / len(shards), largest / len(shards))
        return jnp.repeat(jnp.exp(steps), shape[dim] // blocks).reshape((-1,) + (1,) * (len(shape) - dim - 1))

    level = one(*shards[0])
    for cut in shards[1:]:
        level = level * one(*cut)
    return level


def bell_draw(rng, extent, scale, limit, pieces=(), kind=jnp.bfloat16):
    result = jax.random.normal(rng, extent, jnp.float32) * scale
    if len(pieces) > 0:
        result = shard_levels(rng, extent, pieces, -0.22, 0.18) * result
    return jnp.clip(result, min=-limit, max=limit).astype(kind)


def noise_with(rng, shape, width, bound, shards, heavy, held_as=jnp.bfloat16):
    array = width * jax.random.normal(rng, shape, jnp.float32)
    if shards:
        array = array * shard_levels(rng, shape, shards, -0.22, 0.18)
    return jnp.clip(with_spikes(array, jax.random.fold_in(rng, 3), *heavy), -bound, bound).astype(held_as)


def setup_inputs(seed: int = 0) -> dict:
    key_list = jax.random.split(jax.random.key(seed), 13)
    return {
        "hidden_states": bell_draw(key_list[0], (TOKENS, D), 1.0, 6.0, ((0, 8), (1, 16))),
        "norm_gain": jnp.clip(1.0 + 0.1 * jax.random.normal(key_list[1], (D,), jnp.float32), 0.5, 1.5),
        "norm_bias": bell_draw(key_list[2], (D,), 0.3, 2.0, (), jnp.float32),
        "qkv_weight": bell_draw(key_list[3], (D, 3 * D), (D // 3) ** -0.5, 0.125, ((0, 8), (1, 16))),
        "qkv_bias": bell_draw(key_list[4], (3 * D,), 0.3, 2.0, ((0, 16),)),
        "dense_weight": noise_with(key_list[5], (D, D), (D // 4) ** -0.5, 0.21875, ((0, 16),), (0, 1, 16, 2.0)),
        "dense_bias": bell_draw(key_list[6], (D,), 0.3, 2.0, ((0, 16),)),
        "prefix_keys": draw_prefix_keys(jax.random.fold_in(key_list[12], 71), 0),
        "prefix_values": bell_draw(key_list[8], (GROUPS, PREFIX, D), 1.7, 10.0, ((0, 8), (2, 16))),
        "suffix_len": draw_suffix_len(jax.random.fold_in(key_list[12], 71), 0),
        "request_order": jax.vmap(lambda own: jax.random.permutation(own, GROUPS))(jax.random.split(key_list[10], N_TOK)).reshape((N_TOK, GROUPS)).astype(jnp.int32),
        "group_slot": jax.random.permutation(key_list[11], GROUPS).astype(jnp.int32),
    }


def layer_norm(values_in, gain, shift):
    widened = values_in.astype(jnp.float32)
    center = lax.optimization_barrier(jnp.mean(widened, axis=-1, keepdims=True))
    spread = lax.optimization_barrier(jnp.mean(jnp.square(widened - center), axis=-1, keepdims=True))
    return ((widened - center) * lax.rsqrt(spread + 1e-05) * gain + shift).astype(jnp.bfloat16)

def shard_layout(lengths, ordering, row_count):
    group_count = lengths.shape[0]
    labels = jnp.arange(group_count, dtype=jnp.int32)
    chosen = (ordering[:, None] == labels[None, :]).astype(jnp.int32)
    ranking = lax.optimization_barrier(jnp.sum(labels[:, None] * chosen, axis=0))
    earlier = (ranking[None, :] < ranking[:, None]).astype(jnp.int32)
    starts = lax.optimization_barrier(jnp.sum(earlier * lengths[None, :], axis=1))
    places = jnp.arange(row_count, dtype=jnp.int32)
    member = ((places[:, None] >= starts[None, :]) & (places[:, None] < (starts + lengths)[None, :])).astype(jnp.int32)
    group_of = lax.optimization_barrier(jnp.sum(member * labels[None, :], axis=1))
    within = places - lax.optimization_barrier(jnp.sum(member * starts[None, :], axis=1))
    return (starts, member, group_of, within)

def rotary(tensor, positions, rot_dims):
    half_dims = rot_dims // 2
    inverse = 10000.0 ** (-(jnp.arange(half_dims, dtype=jnp.float32) * 2.0) / rot_dims)
    angles = positions.astype(jnp.float32)[:, None] * inverse[None, :]
    cosine = jnp.cos(angles)[:, None, :]
    sine_part = jnp.sin(angles)[:, None, :]
    lower_half = tensor[..., :half_dims]
    upper_half = tensor[..., half_dims:rot_dims]
    return jnp.concatenate([lower_half * cosine - upper_half * sine_part, upper_half * cosine + lower_half * sine_part, tensor[..., rot_dims:]], axis=-1)

def suffix_part(operands):
    queries, keys_new, values_new, group_of = operands
    scaling = 1.0 / math.sqrt(HS)
    scores = jnp.einsum('ihd,jhd->hij', queries.astype(jnp.float32), keys_new.astype(jnp.float32)) * scaling
    places = jnp.arange(queries.shape[0], dtype=jnp.int32)
    allowed = (group_of[:, None] == group_of[None, :]) & (places[None, :] <= places[:, None])
    masked = jnp.where(allowed[None], scores, -jnp.inf)
    row_peak = lax.optimization_barrier(jnp.max(masked, axis=-1))
    weights = jnp.exp(masked - row_peak[..., None])
    row_mass = lax.optimization_barrier(jnp.sum(weights, axis=-1))
    blended = jnp.einsum('hij,jhd->ihd', weights.astype(jnp.bfloat16).astype(jnp.float32), values_new.astype(jnp.float32)) / jnp.transpose(row_mass)[..., None]
    return (jnp.transpose(row_peak), jnp.transpose(row_mass), blended)

def reference(hidden_states, norm_gain, norm_bias, qkv_weight, qkv_bias, dense_weight, dense_bias, prefix_keys, prefix_values, suffix_len, request_order, group_slot):
    total_rows = hidden_states.shape[0]
    normed = layer_norm(hidden_states, norm_gain, norm_bias)
    projected = jnp.dot(normed, qkv_weight, preferred_element_type=jnp.float32) + qkv_bias.astype(jnp.float32)
    projected = projected.reshape(total_rows, HEADS, 3, HS)

    def layout_rows(lengths, ordering):
        return shard_layout(lengths, ordering, TOK_DEV)
    starts, member, group_of, within = jax.vmap(layout_rows)(suffix_len, request_order)
    positions = (PREFIX + within).reshape(total_rows)
    queries = rotary(projected[:, :, 0], positions, ROT).astype(jnp.bfloat16)
    keys_new = rotary(projected[:, :, 1], positions, ROT).astype(jnp.bfloat16)
    values_new = projected[:, :, 2].astype(jnp.bfloat16)
    suf_peak, suf_mass, suf_out = lax.map(suffix_part, (queries.reshape(N_TOK, TOK_DEV, HEADS, HS), keys_new.reshape(N_TOK, TOK_DEV, HEADS, HS), values_new.reshape(N_TOK, TOK_DEV, HEADS, HS), group_of))
    suf_peak = suf_peak.reshape(total_rows, HEADS)
    suf_mass = suf_mass.reshape(total_rows, HEADS)
    suf_out = suf_out.reshape(total_rows, HEADS, HS)
    shard_ids = jnp.arange(N_TOK, dtype=jnp.int32)
    cap_index = jnp.arange(CAP, dtype=jnp.int32)
    live_slot = cap_index[None, None, :] < jnp.transpose(suffix_len)[:, :, None]
    source_rows = shard_ids[None, :, None] * TOK_DEV + jnp.transpose(starts)[:, :, None] + cap_index[None, None, :]
    source_rows = jnp.where(live_slot, source_rows, 0).astype(jnp.int32)
    gathered = jnp.where(live_slot[..., None, None], queries[source_rows], jnp.zeros((), jnp.bfloat16))
    gathered = gathered.reshape(GROUPS, N_TOK * CAP, HEADS, HS)
    scaling = 1.0 / math.sqrt(HS)

    def one_group(operands):
        group_queries, slot_id = operands
        key_heads = prefix_keys[slot_id].reshape(PREFIX, HEADS, HS).astype(jnp.float32)
        value_heads = prefix_values[slot_id].reshape(PREFIX, HEADS, HS).astype(jnp.float32)
        scores = jnp.einsum('rhd,phd->hrp', group_queries.astype(jnp.float32), key_heads) * scaling
        row_peak = lax.optimization_barrier(jnp.max(scores, axis=-1))
        weights = jnp.exp(scores - row_peak[..., None])
        row_mass = lax.optimization_barrier(jnp.sum(weights, axis=-1))
        blended = jnp.einsum('hrp,phd->rhd', weights.astype(jnp.bfloat16).astype(jnp.float32), value_heads) / jnp.transpose(row_mass)[..., None]
        return (blended, jnp.transpose(row_peak), jnp.transpose(row_mass))
    pre_all, peak_all, mass_all = lax.map(one_group, (gathered, group_slot))
    token_group = group_of.reshape(total_rows)
    token_shard = (jnp.arange(total_rows, dtype=jnp.int32) // TOK_DEV).astype(jnp.int32)
    flat_index = (token_group * (N_TOK * CAP) + token_shard * CAP + within.reshape(total_rows)).astype(jnp.int32)
    pre_out = pre_all.reshape(GROUPS * N_TOK * CAP, HEADS, HS)[flat_index]
    pre_peak = peak_all.reshape(GROUPS * N_TOK * CAP, HEADS)[flat_index]
    pre_mass = mass_all.reshape(GROUPS * N_TOK * CAP, HEADS)[flat_index]
    joint_peak = jnp.maximum(pre_peak, suf_peak)
    pre_share = pre_mass * jnp.exp(pre_peak - joint_peak)
    suf_share = suf_mass * jnp.exp(suf_peak - joint_peak)
    combined = (pre_share[..., None] * pre_out + suf_share[..., None] * suf_out) / (pre_share + suf_share)[..., None]
    attention = combined.reshape(total_rows, D).astype(jnp.bfloat16)
    dense = jnp.dot(attention, dense_weight, preferred_element_type=jnp.float32)
    return (hidden_states.astype(jnp.float32) + dense_bias.astype(jnp.float32) + dense).astype(jnp.bfloat16)
```

```python
import jax
import jax.numpy as jnp
from jax import lax
from jax.sharding import PartitionSpec as P
from jax.experimental import pallas as pl
from jax.experimental.pallas import tpu as pltpu

HS = 96


def layer_norm(values_in, gain, shift):
    widened = values_in.astype(jnp.float32)
    center = jnp.mean(widened, axis=-1, keepdims=True)
    spread = jnp.mean(jnp.square(widened - center), axis=-1, keepdims=True)
    return ((widened - center) * lax.rsqrt(spread + 1e-05) * gain + shift).astype(jnp.bfloat16)


def shard_layout(lengths, ordering, row_count):
    group_count = lengths.shape[0]
    labels = jnp.arange(group_count, dtype=jnp.int32)
    chosen = (ordering[:, None] == labels[None, :]).astype(jnp.int32)
    ranking = jnp.sum(labels[:, None] * chosen, axis=0)
    earlier = (ranking[None, :] < ranking[:, None]).astype(jnp.int32)
    starts = jnp.sum(earlier * lengths[None, :], axis=1)
    places = jnp.arange(row_count, dtype=jnp.int32)
    member = (
        (places[:, None] >= starts[None, :]) & (places[:, None] < (starts + lengths)[None, :])
    ).astype(jnp.int32)
    group_of = jnp.sum(member * labels[None, :], axis=1)
    within = places - jnp.sum(member * starts[None, :], axis=1)
    return (starts, member, group_of, within)


def rotary(tensor, positions, rot_dims):
    half_dims = rot_dims // 2
    inverse = 10000.0 ** (-(jnp.arange(half_dims, dtype=jnp.float32) * 2.0) / rot_dims)
    angles = positions.astype(jnp.float32)[:, None] * inverse[None, :]
    cosine = jnp.cos(angles)[:, None, :]
    sine_part = jnp.sin(angles)[:, None, :]
    lower_half = tensor[..., :half_dims]
    upper_half = tensor[..., half_dims:rot_dims]
    return jnp.concatenate(
        [
            lower_half * cosine - upper_half * sine_part,
            upper_half * cosine + lower_half * sine_part,
            tensor[..., rot_dims:],
        ],
        axis=-1,
    )


def local_suffix(queries, keys_new, values_new, group_of):
    scaling = HS ** (-0.5)
    scores = (
        jnp.einsum("ihd,jhd->hij", queries, keys_new, preferred_element_type=jnp.float32) * scaling
    )
    places = jnp.arange(queries.shape[0], dtype=jnp.int32)
    allowed = (group_of[:, None] == group_of[None, :]) & (places[None, :] <= places[:, None])
    masked = jnp.where(allowed[None], scores, -jnp.inf)
    row_peak = jnp.max(masked, axis=-1)
    weights = jnp.exp(masked - row_peak[..., None])
    row_mass = jnp.sum(weights, axis=-1)
    blended = (
        jnp.einsum(
            "hij,jhd->ihd",
            weights.astype(jnp.bfloat16),
            values_new,
            preferred_element_type=jnp.float32,
        )
        / jnp.transpose(row_mass)[..., None]
    )
    return (jnp.transpose(row_peak), jnp.transpose(row_mass), blended)


def prefix_slot(operands):
    queries_in, keys_in, values_in = operands
    row_total = queries_in.shape[0]
    local_width = queries_in.shape[1]
    local_heads = local_width // HS
    prefix_length = keys_in.shape[0]
    query_heads = queries_in.reshape(row_total, local_heads, HS)
    key_heads = keys_in.reshape(prefix_length, local_heads, HS)
    value_heads = values_in.reshape(prefix_length, local_heads, HS)
    scores = jnp.einsum(
        "rhd,phd->hrp", query_heads, key_heads, preferred_element_type=jnp.float32
    ) * HS ** (-0.5)
    row_peak = jnp.max(scores, axis=-1)
    weights = jnp.exp(scores - row_peak[..., None])
    row_mass = jnp.sum(weights, axis=-1)
    blended = (
        jnp.einsum(
            "hrp,phd->rhd",
            weights.astype(jnp.bfloat16),
            value_heads,
            preferred_element_type=jnp.float32,
        )
        / jnp.transpose(row_mass)[..., None]
    )
    return (
        blended.reshape(row_total, local_width),
        jnp.transpose(row_peak),
        jnp.transpose(row_mass),
    )


def prefix_kernel(q_ref, k_ref, v_ref, o_ref, peak_ref, mass_ref):
    local_heads = q_ref.shape[-1] // HS
    peaks = []
    masses = []
    for head in range(local_heads):
        cols = pl.ds(head * HS, HS)
        scores = lax.dot_general(
            q_ref[:, cols],
            k_ref[:, cols],
            (((1,), (1,)), ((), ())),
            preferred_element_type=jnp.float32,
        ) * HS ** (-0.5)
        row_peak = jnp.max(scores, axis=-1, keepdims=True)
        weights = jnp.exp(scores - row_peak)
        row_mass = jnp.sum(weights, axis=-1, keepdims=True)
        blended = jnp.dot(
            weights.astype(jnp.bfloat16), v_ref[:, cols], preferred_element_type=jnp.float32
        )
        o_ref[:, cols] = blended / row_mass
        peaks.append(row_peak)
        masses.append(row_mass)
    peak_ref[...] = jnp.concatenate(peaks, axis=-1)
    mass_ref[...] = jnp.concatenate(masses, axis=-1)


def prefix_attention(queries_in, keys_in, values_in):
    slot_count, row_total, local_width = queries_in.shape
    prefix_length = keys_in.shape[1]
    local_heads = local_width // HS
    row_tile = row_total // 2 if row_total % 16 == 0 else row_total
    grid = (slot_count, row_total // row_tile)
    return pl.pallas_call(
        prefix_kernel,
        grid=grid,
        in_specs=[
            pl.BlockSpec((None, row_tile, local_width), lambda s, r: (s, r, 0)),
            pl.BlockSpec((None, prefix_length, local_width), lambda s, r: (s, 0, 0)),
            pl.BlockSpec((None, prefix_length, local_width), lambda s, r: (s, 0, 0)),
        ],
        out_specs=[
            pl.BlockSpec((None, row_tile, local_width), lambda s, r: (s, r, 0)),
            pl.BlockSpec((None, row_tile, local_heads), lambda s, r: (s, r, 0)),
            pl.BlockSpec((None, row_tile, local_heads), lambda s, r: (s, r, 0)),
        ],
        out_shape=[
            jax.ShapeDtypeStruct((slot_count, row_total, local_width), jnp.float32),
            jax.ShapeDtypeStruct((slot_count, row_total, local_heads), jnp.float32),
            jax.ShapeDtypeStruct((slot_count, row_total, local_heads), jnp.float32),
        ],
        compiler_params=pltpu.CompilerParams(vmem_limit_bytes=60 * 1024 * 1024),
    )(queries_in, keys_in, values_in)


def on_device(
    hidden_states,
    norm_gain,
    norm_bias,
    qkv_weight,
    qkv_bias,
    dense_weight,
    dense_bias,
    prefix_keys,
    prefix_values,
    suffix_len,
    request_order,
    group_slot,
):
    tok_rows = hidden_states.shape[0]
    slot_local = prefix_keys.shape[0]
    prefix_length = prefix_keys.shape[1]
    local_width = prefix_keys.shape[2]
    local_heads = local_width // HS
    group_count = slot_local * lax.axis_size("tok")
    capacity = 3 * tok_rows // group_count
    full_rows = lax.all_gather(hidden_states, "head", axis=1, tiled=True)
    normed = layer_norm(full_rows, norm_gain, norm_bias)
    projected = jnp.dot(
        normed,
        lax.all_gather(qkv_weight, "tok", axis=0, tiled=True),
        preferred_element_type=jnp.float32,
    )
    projected = (projected + qkv_bias.astype(jnp.float32)).reshape(tok_rows, local_heads, 3, HS)
    lengths = suffix_len[0]
    starts, member, group_of, within = shard_layout(lengths, request_order[0], tok_rows)
    positions = prefix_length + within
    queries = rotary(projected[:, :, 0], positions, HS // 4).astype(jnp.bfloat16)
    keys_new = rotary(projected[:, :, 1], positions, HS // 4).astype(jnp.bfloat16)
    values_new = projected[:, :, 2].astype(jnp.bfloat16)
    suf_peak, suf_mass, suf_out = local_suffix(queries, keys_new, values_new, group_of)
    labels = jnp.arange(group_count, dtype=jnp.int32)
    slot_match = (group_slot[:, None] == labels[None, :]).astype(jnp.int32)
    slot_starts = jnp.sum(starts[:, None] * slot_match, axis=0)
    slot_lengths = jnp.sum(lengths[:, None] * slot_match, axis=0)
    cap_index = jnp.arange(capacity, dtype=jnp.int32)
    live_slot = cap_index[None, :] < slot_lengths[:, None]
    source_rows = jnp.where(live_slot, slot_starts[:, None] + cap_index[None, :], 0)
    flat_query = queries.reshape(tok_rows, local_width)
    outgoing = jnp.where(live_slot[..., None], flat_query[source_rows], jnp.zeros((), jnp.bfloat16))
    incoming = lax.all_to_all(outgoing, "tok", split_axis=0, concat_axis=1, tiled=True)
    pre_all, peak_all, mass_all = prefix_attention(incoming, prefix_keys, prefix_values)
    returned = (
        lax.all_to_all(pre_all, "tok", split_axis=1, concat_axis=0, tiled=True),
        lax.all_to_all(peak_all, "tok", split_axis=1, concat_axis=0, tiled=True),
        lax.all_to_all(mass_all, "tok", split_axis=1, concat_axis=0, tiled=True),
    )
    token_slot = jnp.sum(member * group_slot[None, :], axis=1)
    flat_index = token_slot * capacity + within
    pre_out = returned[0].reshape(group_count * capacity, local_heads, HS)[flat_index]
    pre_peak = returned[1].reshape(group_count * capacity, local_heads)[flat_index]
    pre_mass = returned[2].reshape(group_count * capacity, local_heads)[flat_index]
    joint_peak = jnp.maximum(pre_peak, suf_peak)
    pre_share = pre_mass * jnp.exp(pre_peak - joint_peak)
    suf_share = suf_mass * jnp.exp(suf_peak - joint_peak)
    combined = (pre_share[..., None] * pre_out + suf_share[..., None] * suf_out) / (
        pre_share + suf_share
    )[..., None]
    attention = combined.reshape(tok_rows, local_width).astype(jnp.bfloat16)
    partial_out = jnp.dot(attention, dense_weight, preferred_element_type=jnp.float32)
    summed = lax.psum_scatter(partial_out, "head", scatter_dimension=1, tiled=True)
    return (hidden_states.astype(jnp.float32) + dense_bias.astype(jnp.float32) + summed).astype(
        jnp.bfloat16
    )


def solution(mesh):
    placed = (
        P("tok", "head"),
        P(),
        P(),
        P("tok", "head"),
        P("head"),
        P("head", None),
        P("head"),
        P("tok", None, "head"),
        P("tok", None, "head"),
        P("tok", None),
        P("tok", None),
        P(),
    )
    return jax.shard_map(
        on_device, mesh=mesh, in_specs=placed, out_specs=P("tok", "head"), check_vma=False
    )
```

```python
import jax
import jax.numpy as jnp
from jax import lax
from jax.sharding import PartitionSpec as P
from jax.experimental import pallas as pl
from jax.experimental.pallas import tpu as pltpu

HS = 96


def layer_norm(values_in, gain, shift):
    widened = values_in.astype(jnp.float32)
    center = jnp.mean(widened, axis=-1, keepdims=True)
    spread = jnp.mean(jnp.square(widened - center), axis=-1, keepdims=True)
    return ((widened - center) * lax.rsqrt(spread + 1e-05) * gain + shift).astype(jnp.bfloat16)


def shard_layout(lengths, ordering, row_count):
    group_count = lengths.shape[0]
    labels = jnp.arange(group_count, dtype=jnp.int32)
    chosen = (ordering[:, None] == labels[None, :]).astype(jnp.int32)
    ranking = jnp.sum(labels[:, None] * chosen, axis=0)
    earlier = (ranking[None, :] < ranking[:, None]).astype(jnp.int32)
    starts = jnp.sum(earlier * lengths[None, :], axis=1)
    places = jnp.arange(row_count, dtype=jnp.int32)
    member = (
        (places[:, None] >= starts[None, :]) & (places[:, None] < (starts + lengths)[None, :])
    ).astype(jnp.int32)
    group_of = jnp.sum(member * labels[None, :], axis=1)
    within = places - jnp.sum(member * starts[None, :], axis=1)
    return (starts, member, group_of, within)


def rotary(tensor, positions, rot_dims):
    half_dims = rot_dims // 2
    inverse = 10000.0 ** (-(jnp.arange(half_dims, dtype=jnp.float32) * 2.0) / rot_dims)
    angles = positions.astype(jnp.float32)[:, None] * inverse[None, :]
    cosine = jnp.cos(angles)[:, None, :]
    sine_part = jnp.sin(angles)[:, None, :]
    lower_half = tensor[..., :half_dims]
    upper_half = tensor[..., half_dims:rot_dims]
    return jnp.concatenate(
        [
            lower_half * cosine - upper_half * sine_part,
            upper_half * cosine + lower_half * sine_part,
            tensor[..., rot_dims:],
        ],
        axis=-1,
    )


def local_suffix(queries, keys_new, values_new, group_of):
    scaling = HS ** (-0.5)
    scores = (
        jnp.einsum("ihd,jhd->hij", queries, keys_new, preferred_element_type=jnp.float32) * scaling
    )
    places = jnp.arange(queries.shape[0], dtype=jnp.int32)
    allowed = (group_of[:, None] == group_of[None, :]) & (places[None, :] <= places[:, None])
    masked = jnp.where(allowed[None], scores, -jnp.inf)
    row_peak = jnp.max(masked, axis=-1)
    weights = jnp.exp(masked - row_peak[..., None])
    row_mass = jnp.sum(weights, axis=-1)
    blended = (
        jnp.einsum(
            "hij,jhd->ihd",
            weights.astype(jnp.bfloat16),
            values_new,
            preferred_element_type=jnp.float32,
        )
        / jnp.transpose(row_mass)[..., None]
    )
    return (jnp.transpose(row_peak), jnp.transpose(row_mass), blended)


def prefix_slot(operands):
    queries_in, keys_in, values_in = operands
    row_total = queries_in.shape[0]
    local_width = queries_in.shape[1]
    local_heads = local_width // HS
    prefix_length = keys_in.shape[0]
    query_heads = queries_in.reshape(row_total, local_heads, HS)
    key_heads = keys_in.reshape(prefix_length, local_heads, HS)
    value_heads = values_in.reshape(prefix_length, local_heads, HS)
    scores = jnp.einsum(
        "rhd,phd->hrp", query_heads, key_heads, preferred_element_type=jnp.float32
    ) * HS ** (-0.5)
    row_peak = jnp.max(scores, axis=-1)
    weights = jnp.exp(scores - row_peak[..., None])
    row_mass = jnp.sum(weights, axis=-1)
    blended = (
        jnp.einsum(
            "hrp,phd->rhd",
            weights.astype(jnp.bfloat16),
            value_heads,
            preferred_element_type=jnp.float32,
        )
        / jnp.transpose(row_mass)[..., None]
    )
    return (
        blended.reshape(row_total, local_width),
        jnp.transpose(row_peak),
        jnp.transpose(row_mass),
    )


def prefix_kernel(q_ref, k_ref, v_ref, o_ref, peak_ref, mass_ref):
    local_heads = q_ref.shape[-1] // HS
    peaks = []
    masses = []
    for head in range(local_heads):
        cols = pl.ds(head * HS, HS)
        scores = lax.dot_general(
            q_ref[:, cols],
            k_ref[:, cols],
            (((1,), (1,)), ((), ())),
            preferred_element_type=jnp.float32,
        ) * HS ** (-0.5)
        row_peak = jnp.max(scores, axis=-1, keepdims=True)
        weights = jnp.exp(scores - row_peak)
        row_mass = jnp.sum(weights, axis=-1, keepdims=True)
        blended = jnp.dot(
            weights.astype(jnp.bfloat16), v_ref[:, cols], preferred_element_type=jnp.float32
        )
        o_ref[:, cols] = blended / row_mass
        peaks.append(row_peak)
        masses.append(row_mass)
    peak_ref[...] = jnp.concatenate(peaks, axis=-1)
    mass_ref[...] = jnp.concatenate(masses, axis=-1)


def prefix_attention(queries_in, keys_in, values_in):
    slot_count, row_total, local_width = queries_in.shape
    prefix_length = keys_in.shape[1]
    local_heads = local_width // HS
    row_tile = row_total // 2 if row_total % 16 == 0 else row_total
    grid = (slot_count, row_total // row_tile)
    return pl.pallas_call(
        prefix_kernel,
        grid=grid,
        in_specs=[
            pl.BlockSpec((None, row_tile, local_width), lambda s, r: (s, r, 0)),
            pl.BlockSpec((None, prefix_length, local_width), lambda s, r: (s, 0, 0)),
            pl.BlockSpec((None, prefix_length, local_width), lambda s, r: (s, 0, 0)),
        ],
        out_specs=[
            pl.BlockSpec((None, row_tile, local_width), lambda s, r: (s, r, 0)),
            pl.BlockSpec((None, row_tile, local_heads), lambda s, r: (s, r, 0)),
            pl.BlockSpec((None, row_tile, local_heads), lambda s, r: (s, r, 0)),
        ],
        out_shape=[
            jax.ShapeDtypeStruct((slot_count, row_total, local_width), jnp.float32),
            jax.ShapeDtypeStruct((slot_count, row_total, local_heads), jnp.float32),
            jax.ShapeDtypeStruct((slot_count, row_total, local_heads), jnp.float32),
        ],
        compiler_params=pltpu.CompilerParams(vmem_limit_bytes=60 * 1024 * 1024),
    )(queries_in, keys_in, values_in)


def on_device(
    hidden_states,
    norm_gain,
    norm_bias,
    qkv_weight,
    qkv_bias,
    dense_weight,
    dense_bias,
    prefix_keys,
    prefix_values,
    suffix_len,
    request_order,
    group_slot,
):
    tok_rows = hidden_states.shape[0]
    slot_local = prefix_keys.shape[0]
    prefix_length = prefix_keys.shape[1]
    local_width = prefix_keys.shape[2]
    local_heads = local_width // HS
    group_count = slot_local * lax.axis_size("tok")
    capacity = 3 * tok_rows // group_count
    head_count = lax.axis_size("head")
    copies = jnp.broadcast_to(hidden_states[None], (head_count,) + hidden_states.shape)
    pieces = lax.all_to_all(copies, "head", split_axis=0, concat_axis=0, tiled=True)
    full_rows = jnp.transpose(pieces, (1, 0, 2)).reshape(tok_rows, head_count * local_width)
    normed = layer_norm(full_rows, norm_gain, norm_bias)
    projected = jnp.dot(
        normed,
        lax.all_gather(qkv_weight, "tok", axis=0, tiled=True),
        preferred_element_type=jnp.float32,
    )
    projected = (projected + qkv_bias.astype(jnp.float32)).reshape(tok_rows, local_heads, 3, HS)
    lengths = suffix_len[0]
    starts, member, group_of, within = shard_layout(lengths, request_order[0], tok_rows)
    positions = prefix_length + within
    queries = rotary(projected[:, :, 0], positions, HS // 4).astype(jnp.bfloat16)
    keys_new = rotary(projected[:, :, 1], positions, HS // 4).astype(jnp.bfloat16)
    values_new = projected[:, :, 2].astype(jnp.bfloat16)
    suf_peak, suf_mass, suf_out = local_suffix(queries, keys_new, values_new, group_of)
    labels = jnp.arange(group_count, dtype=jnp.int32)
    slot_match = (group_slot[:, None] == labels[None, :]).astype(jnp.int32)
    slot_starts = jnp.sum(starts[:, None] * slot_match, axis=0)
    slot_lengths = jnp.sum(lengths[:, None] * slot_match, axis=0)
    cap_index = jnp.arange(capacity, dtype=jnp.int32)
    live_slot = cap_index[None, :] < slot_lengths[:, None]
    source_rows = jnp.where(live_slot, slot_starts[:, None] + cap_index[None, :], 0)
    flat_query = queries.reshape(tok_rows, local_width)
    outgoing = jnp.where(live_slot[..., None], flat_query[source_rows], jnp.zeros((), jnp.bfloat16))
    incoming = lax.all_to_all(outgoing, "tok", split_axis=0, concat_axis=1, tiled=True)
    pre_all, peak_all, mass_all = prefix_attention(incoming, prefix_keys, prefix_values)
    returned = (
        lax.all_to_all(pre_all, "tok", split_axis=1, concat_axis=0, tiled=True),
        lax.all_to_all(peak_all, "tok", split_axis=1, concat_axis=0, tiled=True),
        lax.all_to_all(mass_all, "tok", split_axis=1, concat_axis=0, tiled=True),
    )
    token_slot = jnp.sum(member * group_slot[None, :], axis=1)
    flat_index = token_slot * capacity + within
    pre_out = returned[0].reshape(group_count * capacity, local_heads, HS)[flat_index]
    pre_peak = returned[1].reshape(group_count * capacity, local_heads)[flat_index]
    pre_mass = returned[2].reshape(group_count * capacity, local_heads)[flat_index]
    joint_peak = jnp.maximum(pre_peak, suf_peak)
    pre_share = pre_mass * jnp.exp(pre_peak - joint_peak)
    suf_share = suf_mass * jnp.exp(suf_peak - joint_peak)
    combined = (pre_share[..., None] * pre_out + suf_share[..., None] * suf_out) / (
        pre_share + suf_share
    )[..., None]
    attention = combined.reshape(tok_rows, local_width).astype(jnp.bfloat16)
    partial_out = jnp.dot(attention, dense_weight, preferred_element_type=jnp.float32)
    summed = lax.psum_scatter(partial_out, "head", scatter_dimension=1, tiled=True)
    return (hidden_states.astype(jnp.float32) + dense_bias.astype(jnp.float32) + summed).astype(
        jnp.bfloat16
    )


def solution(mesh):
    placed = (
        P("tok", "head"),
        P(),
        P(),
        P("tok", "head"),
        P("head"),
        P("head", None),
        P("head"),
        P("tok", None, "head"),
        P("tok", None, "head"),
        P("tok", None),
        P("tok", None),
        P(),
    )
    return jax.shard_map(
        on_device, mesh=mesh, in_specs=placed, out_specs=P("tok", "head"), check_vma=False
    )
```

```python
import jax
import jax.numpy as jnp
from jax import lax
from jax.sharding import PartitionSpec as P
from jax.experimental import pallas as pl
from jax.experimental.pallas import tpu as pltpu

HS = 96


def layer_norm(values_in, gain, shift):
    widened = values_in.astype(jnp.float32)
    center = jnp.mean(widened, axis=-1, keepdims=True)
    spread = jnp.mean(jnp.square(widened - center), axis=-1, keepdims=True)
    return ((widened - center) * lax.rsqrt(spread + 1e-05) * gain + shift).astype(jnp.bfloat16)


def shard_layout(lengths, ordering, row_count):
    group_count = lengths.shape[0]
    labels = jnp.arange(group_count, dtype=jnp.int32)
    chosen = (ordering[:, None] == labels[None, :]).astype(jnp.int32)
    ranking = jnp.sum(labels[:, None] * chosen, axis=0)
    earlier = (ranking[None, :] < ranking[:, None]).astype(jnp.int32)
    starts = jnp.sum(earlier * lengths[None, :], axis=1)
    places = jnp.arange(row_count, dtype=jnp.int32)
    member = (
        (places[:, None] >= starts[None, :]) & (places[:, None] < (starts + lengths)[None, :])
    ).astype(jnp.int32)
    group_of = jnp.sum(member * labels[None, :], axis=1)
    within = places - jnp.sum(member * starts[None, :], axis=1)
    return (starts, member, group_of, within)


def rotary(tensor, positions, rot_dims):
    half_dims = rot_dims // 2
    inverse = 10000.0 ** (-(jnp.arange(half_dims, dtype=jnp.float32) * 2.0) / rot_dims)
    angles = positions.astype(jnp.float32)[:, None] * inverse[None, :]
    cosine = jnp.cos(angles)[:, None, :]
    sine_part = jnp.sin(angles)[:, None, :]
    lower_half = tensor[..., :half_dims]
    upper_half = tensor[..., half_dims:rot_dims]
    return jnp.concatenate(
        [
            lower_half * cosine - upper_half * sine_part,
            upper_half * cosine + lower_half * sine_part,
            tensor[..., rot_dims:],
        ],
        axis=-1,
    )


def local_suffix(queries, keys_new, values_new, group_of):
    scaling = HS ** (-0.5)
    scores = (
        jnp.einsum("ihd,jhd->hij", queries, keys_new, preferred_element_type=jnp.float32) * scaling
    )
    places = jnp.arange(queries.shape[0], dtype=jnp.int32)
    allowed = (group_of[:, None] == group_of[None, :]) & (places[None, :] <= places[:, None])
    masked = jnp.where(allowed[None], scores, -jnp.inf)
    row_peak = jnp.max(masked, axis=-1)
    weights = jnp.exp(masked - row_peak[..., None])
    row_mass = jnp.sum(weights, axis=-1)
    blended = (
        jnp.einsum(
            "hij,jhd->ihd",
            weights.astype(jnp.bfloat16),
            values_new,
            preferred_element_type=jnp.float32,
        )
        / jnp.transpose(row_mass)[..., None]
    )
    return (jnp.transpose(row_peak), jnp.transpose(row_mass), blended)


def prefix_slot(operands):
    queries_in, keys_in, values_in = operands
    row_total = queries_in.shape[0]
    local_width = queries_in.shape[1]
    local_heads = local_width // HS
    prefix_length = keys_in.shape[0]
    query_heads = queries_in.reshape(row_total, local_heads, HS)
    key_heads = keys_in.reshape(prefix_length, local_heads, HS)
    value_heads = values_in.reshape(prefix_length, local_heads, HS)
    scores = jnp.einsum(
        "rhd,phd->hrp", query_heads, key_heads, preferred_element_type=jnp.float32
    ) * HS ** (-0.5)
    row_peak = jnp.max(scores, axis=-1)
    weights = jnp.exp(scores - row_peak[..., None])
    row_mass = jnp.sum(weights, axis=-1)
    blended = (
        jnp.einsum(
            "hrp,phd->rhd",
            weights.astype(jnp.bfloat16),
            value_heads,
            preferred_element_type=jnp.float32,
        )
        / jnp.transpose(row_mass)[..., None]
    )
    return (
        blended.reshape(row_total, local_width),
        jnp.transpose(row_peak),
        jnp.transpose(row_mass),
    )


def prefix_kernel(q_ref, k_ref, v_ref, o_ref, peak_ref, mass_ref):
    local_heads = q_ref.shape[-1] // HS
    peaks = []
    masses = []
    for head in range(local_heads):
        cols = pl.ds(head * HS, HS)
        scores = lax.dot_general(
            q_ref[:, cols],
            k_ref[:, cols],
            (((1,), (1,)), ((), ())),
            preferred_element_type=jnp.float32,
        ) * HS ** (-0.5)
        row_peak = jnp.max(scores, axis=-1, keepdims=True)
        weights = jnp.exp(scores - row_peak)
        row_mass = jnp.sum(weights, axis=-1, keepdims=True)
        blended = jnp.dot(
            weights.astype(jnp.bfloat16), v_ref[:, cols], preferred_element_type=jnp.float32
        )
        o_ref[:, cols] = blended / row_mass
        peaks.append(row_peak)
        masses.append(row_mass)
    peak_ref[...] = jnp.concatenate(peaks, axis=-1)
    mass_ref[...] = jnp.concatenate(masses, axis=-1)


def prefix_attention(queries_in, keys_in, values_in):
    slot_count, row_total, local_width = queries_in.shape
    prefix_length = keys_in.shape[1]
    local_heads = local_width // HS
    row_tile = row_total // 2 if row_total % 16 == 0 else row_total
    grid = (slot_count, row_total // row_tile)
    return pl.pallas_call(
        prefix_kernel,
        grid=grid,
        in_specs=[
            pl.BlockSpec((None, row_tile, local_width), lambda s, r: (s, r, 0)),
            pl.BlockSpec((None, prefix_length, local_width), lambda s, r: (s, 0, 0)),
            pl.BlockSpec((None, prefix_length, local_width), lambda s, r: (s, 0, 0)),
        ],
        out_specs=[
            pl.BlockSpec((None, row_tile, local_width), lambda s, r: (s, r, 0)),
            pl.BlockSpec((None, row_tile, local_heads), lambda s, r: (s, r, 0)),
            pl.BlockSpec((None, row_tile, local_heads), lambda s, r: (s, r, 0)),
        ],
        out_shape=[
            jax.ShapeDtypeStruct((slot_count, row_total, local_width), jnp.float32),
            jax.ShapeDtypeStruct((slot_count, row_total, local_heads), jnp.float32),
            jax.ShapeDtypeStruct((slot_count, row_total, local_heads), jnp.float32),
        ],
        compiler_params=pltpu.CompilerParams(vmem_limit_bytes=60 * 1024 * 1024),
    )(queries_in, keys_in, values_in)


def on_device(
    hidden_states,
    norm_gain,
    norm_bias,
    qkv_weight,
    qkv_bias,
    dense_weight,
    dense_bias,
    prefix_keys,
    prefix_values,
    suffix_len,
    request_order,
    group_slot,
):
    tok_rows = hidden_states.shape[0]
    slot_local = prefix_keys.shape[0]
    prefix_length = prefix_keys.shape[1]
    local_width = prefix_keys.shape[2]
    local_heads = local_width // HS
    group_count = slot_local * lax.axis_size("tok")
    capacity = 3 * tok_rows // group_count
    full_rows = lax.all_gather(hidden_states, "head", axis=1, tiled=True)
    normed = layer_norm(full_rows, norm_gain, norm_bias)
    projected = jnp.dot(
        normed,
        lax.all_gather(qkv_weight, "tok", axis=0, tiled=True),
        preferred_element_type=jnp.float32,
    )
    projected = (projected + qkv_bias.astype(jnp.float32)).reshape(tok_rows, local_heads, 3, HS)
    lengths = suffix_len[0]
    starts, member, group_of, within = shard_layout(lengths, request_order[0], tok_rows)
    positions = prefix_length + within
    queries = rotary(projected[:, :, 0], positions, HS // 4).astype(jnp.bfloat16)
    keys_new = rotary(projected[:, :, 1], positions, HS // 4).astype(jnp.bfloat16)
    values_new = projected[:, :, 2].astype(jnp.bfloat16)
    suf_peak, suf_mass, suf_out = local_suffix(queries, keys_new, values_new, group_of)
    labels = jnp.arange(group_count, dtype=jnp.int32)
    slot_match = (group_slot[:, None] == labels[None, :]).astype(jnp.int32)
    slot_starts = jnp.sum(starts[:, None] * slot_match, axis=0)
    slot_lengths = jnp.sum(lengths[:, None] * slot_match, axis=0)
    cap_index = jnp.arange(capacity, dtype=jnp.int32)
    live_slot = cap_index[None, :] < slot_lengths[:, None]
    source_rows = jnp.where(live_slot, slot_starts[:, None] + cap_index[None, :], 0)
    flat_query = queries.reshape(tok_rows, local_width)
    outgoing = jnp.where(live_slot[..., None], flat_query[source_rows], jnp.zeros((), jnp.bfloat16))
    incoming = lax.all_to_all(outgoing, "tok", split_axis=0, concat_axis=1, tiled=True)
    pre_all, peak_all, mass_all = prefix_attention(incoming, prefix_keys, prefix_values)
    returned = (
        lax.all_to_all(pre_all, "tok", split_axis=1, concat_axis=0, tiled=True),
        lax.all_to_all(peak_all, "tok", split_axis=1, concat_axis=0, tiled=True),
        lax.all_to_all(mass_all, "tok", split_axis=1, concat_axis=0, tiled=True),
    )
    token_slot = jnp.sum(member * group_slot[None, :], axis=1)
    flat_index = token_slot * capacity + within
    pre_out = returned[0].reshape(group_count * capacity, local_heads, HS)[flat_index]
    pre_peak = returned[1].reshape(group_count * capacity, local_heads)[flat_index]
    pre_mass = returned[2].reshape(group_count * capacity, local_heads)[flat_index]
    joint_peak = jnp.maximum(pre_peak, suf_peak)
    pre_share = pre_mass * jnp.exp(pre_peak - joint_peak)
    suf_share = suf_mass * jnp.exp(suf_peak - joint_peak)
    combined = (pre_share[..., None] * pre_out + suf_share[..., None] * suf_out) / (
        pre_share + suf_share
    )[..., None]
    attention = combined.reshape(tok_rows, local_width).astype(jnp.bfloat16)
    partial_out = jnp.dot(attention, dense_weight, preferred_element_type=jnp.float32)
    summed = lax.psum_scatter(
        partial_out.astype(jnp.bfloat16), "head", scatter_dimension=1, tiled=True
    ).astype(jnp.float32)
    return (hidden_states.astype(jnp.float32) + dense_bias.astype(jnp.float32) + summed).astype(
        jnp.bfloat16
    )


def solution(mesh):
    placed = (
        P("tok", "head"),
        P(),
        P(),
        P("tok", "head"),
        P("head"),
        P("head", None),
        P("head"),
        P("tok", None, "head"),
        P("tok", None, "head"),
        P("tok", None),
        P("tok", None),
        P(),
    )
    return jax.shard_map(
        on_device, mesh=mesh, in_specs=placed, out_specs=P("tok", "head"), check_vma=False
    )
```
